512 devices in a mesh: seq: 32 (over x, z), head: 16 (over y, core).
Axes of the slice: x: 4, y: 8, z: 8, core: 2. Of those that a mesh axis runs over, the one named last changes fastest.
Arguments:
- queries: bfloat16 [65536, 4096], P(('seq', 'head')), may hold values from -100 to 100
- keys: bfloat16 [65536, 4096], P(('seq', 'head')), may hold values from -6 to 6
- values: bfloat16 [65536, 4096], P(('seq', 'head')), may hold values from -6 to 6
- doc_blocks: int32 [8], replicated, may hold values from 1 to 256, 512 in all
Outputs:
- attended: bfloat16 [65536, 4096], P(('seq', 'head'))
The draws below stay inside these ranges and needn't reach their ends.
Inputs may be any that keep to these rules, and one draw needn't show every extreme that they name: `doc_blocks`: the 8 lengths sum to 512; the longest is 256.
All inputs are finite; a program needn't handle non-finite values.
Results may differ from the reference program's by a relative error of at most 0.0031.
Values may be sent and summed in bfloat16 or wider, within the bound.
No kernel may reach another device: no remote copies, remote signals or barrier semaphores. Data moves between devices by JAX's collectives and lax.ppermute only.
A program may use at most 64 MiB of HBM per device.

```python
import math
import jax
import jax.numpy as jnp
import numpy as np
from jax import lax

H = 32
DH = 128
BLOCK = 128
NDOC = 8
TOKENS = 65536
STRETCH = 2048
NBLK = 512
N_SEQ = 32


def query_key_pair(key):
    shape = (TOKENS, H * DH)
    query_out = jnp.clip(jax.random.normal(jax.random.fold_in(key, 11), shape, jnp.float32), -6.0, 6.0)
    key_out = jnp.clip(jax.random.normal(jax.random.fold_in(key, 12), shape, jnp.float32), -6.0, 6.0)
    return (query_out, key_out)


def draw_queries(key, part):
    return query_key_pair(key)[0].astype(jnp.bfloat16)


def draw_keys(key, part):
    return query_key_pair(key)[1].astype(jnp.bfloat16)


def block_scale(rng, shape, shards, least, largest):
    level, own = 1.0, jax.random.fold_in(rng, 6)
    for dim, blocks in shards:
        draws = jnp.exp(jax.random.uniform(jax.random.fold_in(own, dim), (blocks,), jnp.float32, least / len(shards), largest / len(shards)))
        level = level * jnp.repeat(draws, shape[dim] // blocks).reshape([-1 if axis == dim else 1 for axis in range(len(shape))])
    return level


def split_up(count, total, limit, slope):
    portions = [(1 << 20) // math.isqrt(standing ** slope) + 1 for standing in range(2, count + 1)]
    surplus, counts = total - limit - (count - 1), [1] * (count - 1)
    while surplus > 0:
        candidates = [i for i in range(count - 1) if counts[i] < limit]
        mass, budget = sum([portions[i] for i in candidates]), surplus
        for i in candidates:
            more = min(limit - counts[i], max(1, budget * portions[i] // mass), surplus)
            counts[i] = counts[i] + more
            surplus = surplus - more
    return np.array([limit] + counts)


def ragged_sizes(rng, amount, total, most, skew):
    if amount == 2:
        one = jax.random.randint(rng, (), max(1, total - most), min(most, total - 1) + 1)
        return jnp.stack([one, total - one])
    tallies = jnp.asarray(split_up(amount, total, most, skew), jnp.int32)
    twos = (amount - 1) // 2
    donor, receiver = tallies[1:1 + 2 * twos:2], tallies[2:2 + 2 * twos:2]
    margin = jnp.minimum(donor - 1, most - receiver)
    shifted = jax.random.randint(jax.random.fold_in(rng, 1), (twos,), 0, 1 << 20) % (margin + 1)
    tallies = tallies.at[1:1 + 2 * twos:2].set(donor - shifted).at[2:2 + 2 * twos:2].set(receiver + shifted)
    return tallies[jax.random.permutation(jax.random.fold_in(rng, 2), amount)]


def normal_values(own_key, shape, scale, limit, cuts=(), kind=jnp.bfloat16):
    entries = scale * jax.random.normal(own_key, shape, jnp.float32)
    if cuts:
        entries = entries * block_scale(own_key, shape, cuts, -0.22, 0.18)
    return jnp.clip(entries, -limit, limit).astype(kind)


def setup_inputs(seed: int = 0) -> dict:
    arg_keys = jax.random.split(jax.random.key(seed), 5)
    return {
        "queries": draw_queries(jax.random.fold_in(arg_keys[4], 71), 0),
        "keys": draw_keys(jax.random.fold_in(arg_keys[4], 71), 0),
        "values": normal_values(arg_keys[2], (TOKENS, H * DH), 1.0, 6.0, ((0, 512),)),
        "doc_blocks": ragged_sizes(arg_keys[3], NDOC, NBLK, NBLK // 2, 2).astype(jnp.int32),
    }


def doc_index(positions, doc_blocks):
    doc_ends = (jnp.cumsum(doc_blocks) * BLOCK).astype(jnp.int32)
    return lax.optimization_barrier(jnp.sum((positions[:, None].astype(jnp.int32) >= doc_ends[None, :-1]).astype(jnp.int32), axis=1)).astype(jnp.int32)

def softmax_part(query_rows, key_rows, value_rows, doc_here):
    stretch_len = query_rows.shape[0]
    row_block = min(512, stretch_len)
    inv_root = DH ** (-0.5)
    key_float = key_rows.astype(jnp.float32)
    value_float = value_rows.astype(jnp.float32)
    key_pos = jnp.arange(stretch_len, dtype=jnp.int32)

    def score_block(index):
        first = (index * row_block).astype(jnp.int32)
        query_block = lax.dynamic_slice_in_dim(query_rows, first, row_block, 0).astype(jnp.float32)
        doc_block = lax.dynamic_slice_in_dim(doc_here, first, row_block, 0)
        query_pos = first + jnp.arange(row_block, dtype=jnp.int32)
        scores = jnp.einsum('qhd,khd->hqk', query_block, key_float, precision=lax.Precision.HIGHEST) * inv_root
        allowed = (key_pos[None, :] <= query_pos[:, None]) & (doc_here[None, :] == doc_block[:, None])
        scores = jnp.where(allowed[None], scores, -1e+30)
        peak = lax.optimization_barrier(jnp.max(scores, axis=-1, keepdims=True))
        expo = jnp.exp(scores - peak)
        weights = (expo / lax.optimization_barrier(jnp.sum(expo, axis=-1, keepdims=True))).astype(jnp.bfloat16)
        return jnp.einsum('hqk,khd->qhd', weights.astype(jnp.float32), value_float, precision=lax.Precision.HIGHEST)
    blocks = lax.map(score_block, jnp.arange(stretch_len // row_block, dtype=jnp.int32))
    return blocks.reshape(stretch_len, query_rows.shape[1], DH)

def reference(queries, keys, values, doc_blocks):
    doc_all = doc_index(jnp.arange(TOKENS, dtype=jnp.int32), doc_blocks).reshape(N_SEQ, STRETCH)
    query_all = queries.reshape(N_SEQ, STRETCH, H, DH)
    key_all = keys.reshape(N_SEQ, STRETCH, H, DH)
    value_all = values.reshape(N_SEQ, STRETCH, H, DH)

    def carry_step(state, inputs):
        running, prev_last = state
        key_stretch, value_stretch, doc_stretch = inputs
        prefix = jnp.where(doc_stretch[0] == prev_last, running, jnp.zeros_like(running))
        tail = (doc_stretch == doc_stretch[-1]).astype(jnp.float32)[:, None, None]
        increment = jnp.einsum('lhd,lhe->hde', key_stretch.astype(jnp.float32) * tail, value_stretch.astype(jnp.float32), precision=lax.Precision.HIGHEST)
        kept = jnp.where(prev_last == doc_stretch[-1], running, jnp.zeros_like(running))
        new_running = (increment + kept).astype(jnp.float32)
        return ((new_running, doc_stretch[-1].astype(jnp.int32)), prefix)
    start_state = (jnp.zeros((H, DH, DH), jnp.float32), jnp.array(-1, dtype=jnp.int32))
    unused, prefixes = lax.scan(carry_step, start_state, (key_all, value_all, doc_all))

    def stretch_out(inputs):
        query_stretch, key_stretch, value_stretch, doc_stretch, prefix = inputs
        linear = jnp.einsum('lhd,hde->lhe', query_stretch.astype(jnp.float32), prefix, precision=lax.Precision.HIGHEST)
        normed = linear * lax.rsqrt(lax.optimization_barrier(jnp.mean(linear * linear, axis=-1, keepdims=True)) + 1e-06)
        normed = normed * (doc_stretch == doc_stretch[0]).astype(jnp.float32)[:, None, None]
        soft = softmax_part(query_stretch, key_stretch, value_stretch, doc_stretch)
        return (soft + normed).astype(jnp.bfloat16)
    outputs = lax.map(stretch_out, (query_all, key_all, value_all, doc_all, prefixes))
    return outputs.reshape(TOKENS, H * DH)
```

```python
import functools
import math

import jax
import jax.numpy as jnp
from jax import lax
from jax.experimental import pallas as pl
from jax.experimental.pallas import tpu as pltpu
from jax.sharding import PartitionSpec as P

H = 32
DH = 128
BLOCK = 128
NDOC = 8
N_HEAD = 16
N_SEQ = 32
HERE = 128
SPAN = HERE * N_HEAD
PAIR = (H // N_HEAD) * DH
ROWS = 256
BIG = 1e30
SCALE = math.log2(math.e) / math.sqrt(DH)

VMEM = pl.BlockSpec(memory_space=pltpu.VMEM)
SMEM = pl.BlockSpec(memory_space=pltpu.SMEM)


def pack_body(*refs):
    *sources, out = refs
    for device in range(N_HEAD):
        for place, source in enumerate(sources):
            out[device, :, place * PAIR : (place + 1) * PAIR] = source[
                :, device * PAIR : (device + 1) * PAIR
            ]


def pack(*tensors):
    step = 32
    width = PAIR * len(tensors)
    return pl.pallas_call(
        pack_body,
        grid=(HERE // step,),
        out_shape=jax.ShapeDtypeStruct((N_HEAD, HERE, width), jnp.bfloat16),
        in_specs=[pl.BlockSpec((step, H * DH), lambda i: (i, 0))] * len(tensors),
        out_specs=pl.BlockSpec((N_HEAD, step, width), lambda i: (0, i, 0)),
        name="pack",
    )(*tensors)


def to_heads(packed):
    got = lax.all_to_all(packed, "head", split_axis=0, concat_axis=0, tiled=True)
    return got.reshape(SPAN, packed.shape[2])


def softmax_body(base_ref, blocks_ref, q_ref, k_ref, v_ref, o_ref, qc, kc, vc):
    base = base_ref[0]
    lane = lax.broadcasted_iota(jnp.int32, (1, DH), 1)
    starts = jnp.full((1, DH), 1 << 30, jnp.int32)
    ends = jnp.full((1, DH), 1 << 30, jnp.int32)
    total = jnp.int32(0)
    for doc in range(NDOC):
        starts = jnp.where(lane == doc, total - base, starts)
        total = total + blocks_ref[doc] * BLOCK
        ends = jnp.where(lane == doc, total - base, ends)
    token = lax.broadcasted_iota(jnp.int32, (SPAN, DH), 0)
    inside = (token >= starts) & (token < ends)
    outside = (token < starts) | (token >= ends)
    real = lax.broadcasted_iota(jnp.int32, (SPAN, DH), 1) < NDOC
    qc[:, DH:] = jnp.where(inside, 1.0, 0.0).astype(jnp.bfloat16)
    kc[:, DH:] = jnp.where(outside & real, -BIG, 0.0).astype(jnp.bfloat16)
    qc[:, :DH] = q_ref[...]
    kc[:, :DH] = k_ref[...]
    vc[:, :DH] = v_ref[...]
    vc[:, DH:] = jnp.ones((SPAN, DH), jnp.bfloat16)
    causal = lax.broadcasted_iota(jnp.int32, (ROWS, ROWS), 1) <= lax.broadcasted_iota(
        jnp.int32, (ROWS, ROWS), 0
    )
    for block in range(SPAN // ROWS):
        first, last = block * ROWS, (block + 1) * ROWS
        scores = lax.dot_general(
            qc[first:last, :],
            kc[:last, :],
            (((1,), (1,)), ((), ())),
            preferred_element_type=jnp.float32,
        )
        corner = jnp.where(causal, scores[:, first:], -BIG)
        scores = jnp.concatenate([scores[:, :first], corner], axis=1) if block else corner
        peak = jnp.max(scores, axis=1, keepdims=True)
        expo = jnp.exp2((scores - peak) * SCALE).astype(jnp.bfloat16)
        summed = jnp.dot(expo, vc[:last, :], preferred_element_type=jnp.float32)
        o_ref[first:last, :] = summed[:, :DH] / summed[:, DH:]


def softmax_part(base, doc_blocks, query_rows, key_value_rows):
    return pl.pallas_call(
        softmax_body,
        grid=(PAIR // DH,),
        out_shape=jax.ShapeDtypeStruct((SPAN, PAIR), jnp.float32),
        in_specs=[
            SMEM,
            SMEM,
            pl.BlockSpec((SPAN, DH), lambda h: (0, h)),
            pl.BlockSpec((SPAN, DH), lambda h: (0, h)),
            pl.BlockSpec((SPAN, DH), lambda h: (0, h + PAIR // DH)),
        ],
        out_specs=pl.BlockSpec((SPAN, DH), lambda h: (0, h)),
        scratch_shapes=[pltpu.VMEM((SPAN, 2 * DH), jnp.bfloat16)] * 3,
        cost_estimate=pl.CostEstimate(
            flops=4 * SPAN * SPAN * PAIR,
            bytes_accessed=SPAN * PAIR * 10,
            transcendentals=SPAN * SPAN,
        ),
        name="softmax",
    )(base, doc_blocks, query_rows, key_value_rows, key_value_rows)


def join_body(limit_ref, q_ref, soft_ref, state_ref, o_ref):
    state = state_ref[...]
    high = state.astype(jnp.bfloat16)
    low = (state - high.astype(jnp.float32)).astype(jnp.bfloat16)
    both = jnp.concatenate([high, low], axis=1)
    parts = jnp.dot(q_ref[...], both, preferred_element_type=jnp.float32)
    linear = parts[:, :DH] + parts[:, DH:]
    normed = linear * lax.rsqrt(jnp.mean(linear * linear, axis=1, keepdims=True) + 1e-06)
    token = pl.program_id(1) * o_ref.shape[0] + lax.broadcasted_iota(jnp.int32, linear.shape, 0)
    normed = jnp.where(token < limit_ref[0], normed, 0.0)
    o_ref[...] = (soft_ref[...] + normed).astype(jnp.bfloat16)


def join(limit, query_rows, soft, state):
    step = 1024
    tile = pl.BlockSpec((step, DH), lambda h, i: (i, h))
    return pl.pallas_call(
        join_body,
        grid=(PAIR // DH, SPAN // step),
        out_shape=jax.ShapeDtypeStruct((SPAN, PAIR), jnp.bfloat16),
        in_specs=[SMEM, tile, tile, pl.BlockSpec((DH, DH), lambda h, i: (h, 0))],
        out_specs=tile,
        cost_estimate=pl.CostEstimate(
            flops=4 * SPAN * PAIR * DH, bytes_accessed=SPAN * PAIR * 8, transcendentals=0
        ),
        name="join",
    )(limit, query_rows, soft, state)


def increment_body(base_ref, blocks_ref, k_ref, v_ref, o_ref):
    start = jnp.int32(0)
    total = jnp.int32(0)
    for doc in range(NDOC - 1):
        total = total + blocks_ref[doc] * BLOCK
        start = jnp.where(total - base_ref[0] < SPAN, total, start)
    token = lax.broadcasted_iota(jnp.int32, (SPAN, DH), 0)
    zero = jnp.zeros((SPAN, DH), jnp.bfloat16)
    tail = jnp.where(token >= start - base_ref[0], k_ref[...], zero)
    o_ref[...] = lax.dot_general(
        tail, v_ref[...], (((0,), (0,)), ((), ())), preferred_element_type=jnp.float32
    )


def increment(base, doc_blocks, key_value_rows):
    return pl.pallas_call(
        increment_body,
        grid=(PAIR // DH,),
        out_shape=jax.ShapeDtypeStruct((PAIR, DH), jnp.float32),
        in_specs=[
            SMEM,
            SMEM,
            pl.BlockSpec((SPAN, DH), lambda h: (0, h)),
            pl.BlockSpec((SPAN, DH), lambda h: (0, h + PAIR // DH)),
        ],
        out_specs=pl.BlockSpec((DH, DH), lambda h: (h, 0)),
        cost_estimate=pl.CostEstimate(
            flops=2 * SPAN * PAIR * DH, bytes_accessed=SPAN * PAIR * 4, transcendentals=0
        ),
        name="increment",
    )(base, doc_blocks, key_value_rows, key_value_rows)


def on_device(queries, keys, values, doc_blocks):
    me = lax.axis_index("seq").astype(jnp.int32)
    base = me * SPAN
    key_value = to_heads(pack(keys, values))
    query_rows = to_heads(pack(queries))

    spans = jnp.arange(N_SEQ, dtype=jnp.int32)
    before = jnp.arange(NDOC)[None, :] <= jnp.arange(NDOC)[:, None]
    ends = jnp.sum(jnp.where(before, doc_blocks[None, :], 0), axis=1) * BLOCK

    def doc_of(token):
        return jnp.sum((token >= ends[:-1]).astype(jnp.int32))

    last = doc_of(base + SPAN - 1)
    first = doc_of(base)
    first_end = jnp.min(jnp.where(jnp.arange(NDOC) >= first, ends, TOKENS_END))

    own = increment(base[None], doc_blocks, key_value)

    def from_back(value, back):
        return lax.ppermute(value, "seq", [(c, c + back) for c in range(N_SEQ - back)])

    def gather(value, backs, doc, start):
        total = start
        for back in backs:
            there = doc_of(base - back * SPAN + SPAN - 1)
            joined = (me >= back) & (there == doc)
            term = jnp.where(joined, from_back(value, back), 0.0)
            total = term if total is None else total + term
        return total

    four = gather(own, (1, 8, 9), last, own)
    state = gather(four, (1, 3, 5, 7), first, None)

    soft = softmax_part(base[None], doc_blocks, query_rows, key_value)
    mixed = join((first_end - base)[None], query_rows, soft, state)
    result = lax.all_to_all(
        mixed.reshape(N_HEAD, HERE, PAIR), "head", split_axis=0, concat_axis=0, tiled=True
    )
    return result.transpose(1, 0, 2).reshape(HERE, H * DH)


TOKENS_END = N_SEQ * SPAN


def solution(mesh):
    placed = (P(("seq", "head"), None), P(("seq", "head"), None), P(("seq", "head"), None), P())
    return jax.shard_map(
        on_device, mesh=mesh, in_specs=placed, out_specs=P(("seq", "head"), None), check_vma=False
    )
```

```python
import functools
import math

import jax
import jax.numpy as jnp
from jax import lax
from jax.experimental import pallas as pl
from jax.experimental.pallas import tpu as pltpu
from jax.sharding import PartitionSpec as P

H = 32
DH = 128
BLOCK = 128
NDOC = 8
N_HEAD = 16
N_SEQ = 32
HERE = 128
SPAN = HERE * N_HEAD
PAIR = (H // N_HEAD) * DH
ROWS = 512
BIG = 1e30
LIMIT = 24 << 20
SCALE = math.log2(math.e) / math.sqrt(DH)

VMEM = pl.BlockSpec(memory_space=pltpu.VMEM)
SMEM = pl.BlockSpec(memory_space=pltpu.SMEM)


def pack_body(count, *refs):
    sources, out, held, in_sem, out_sem = refs[:count], refs[count], *refs[count + 1 :]
    taken = [
        [
            pltpu.make_async_copy(
                source.at[:, device * PAIR : (device + 1) * PAIR],
                held.at[device, :, place * PAIR : (place + 1) * PAIR],
                in_sem.at[place, device],
            )
            for place, source in enumerate(sources)
        ]
        for device in range(N_HEAD)
    ]
    put = [
        pltpu.make_async_copy(held.at[device], out.at[device], out_sem.at[device])
        for device in range(N_HEAD)
    ]
    for copies in taken:
        for copy in copies:
            copy.start()
    for copies, copy in zip(taken, put):
        for one in copies:
            one.wait()
        copy.start()
    for copy in put:
        copy.wait()


def pack(*tensors):
    count = len(tensors)
    shape = (N_HEAD, HERE, PAIR * count)
    return pl.pallas_call(
        functools.partial(pack_body, count),
        out_shape=jax.ShapeDtypeStruct(shape, jnp.bfloat16),
        in_specs=[pl.BlockSpec(memory_space=pl.ANY)] * count,
        out_specs=pl.BlockSpec(memory_space=pl.ANY),
        scratch_shapes=[
            pltpu.VMEM(shape, jnp.bfloat16),
            pltpu.SemaphoreType.DMA((count, N_HEAD)),
            pltpu.SemaphoreType.DMA((N_HEAD,)),
        ],
        name="pack",
    )(*tensors)


def to_heads(packed):
    got = lax.all_to_all(packed, "head", split_axis=0, concat_axis=0, tiled=True)
    return got.reshape(SPAN, packed.shape[2])


def softmax_body(base_ref, blocks_ref, q_ref, k_ref, v_ref, o_ref, qc, kc, vc):
    base = base_ref[0]
    lane = lax.broadcasted_iota(jnp.int32, (1, DH), 1)
    starts = jnp.full((1, DH), 1 << 30, jnp.int32)
    ends = jnp.full((1, DH), 1 << 30, jnp.int32)
    total = jnp.int32(0)
    for doc in range(NDOC):
        starts = jnp.where(lane == doc, total - base, starts)
        total = total + blocks_ref[doc] * BLOCK
        ends = jnp.where(lane == doc, total - base, ends)
    token = lax.broadcasted_iota(jnp.int32, (SPAN, DH), 0)
    inside = (token >= starts) & (token < ends)
    outside = (token < starts) | (token >= ends)
    real = lax.broadcasted_iota(jnp.int32, (SPAN, DH), 1) < NDOC
    qc[:, DH:] = jnp.where(inside, 1.0, 0.0).astype(jnp.bfloat16)
    kc[:, DH:] = jnp.where(outside & real, -BIG, 0.0).astype(jnp.bfloat16)
    qc[:, :DH] = q_ref[...]
    kc[:, :DH] = k_ref[...]
    vc[:, :DH] = v_ref[...]
    vc[:, DH:] = jnp.ones((SPAN, DH), jnp.bfloat16)
    causal = lax.broadcasted_iota(jnp.int32, (ROWS, ROWS), 1) <= lax.broadcasted_iota(
        jnp.int32, (ROWS, ROWS), 0
    )
    for block in range(SPAN // ROWS):
        first, last = block * ROWS, (block + 1) * ROWS
        scores = lax.dot_general(
            qc[first:last, :],
            kc[:last, :],
            (((1,), (1,)), ((), ())),
            preferred_element_type=jnp.float32,
        )
        corner = jnp.where(causal, scores[:, first:], -BIG)
        peak = jnp.max(corner, axis=1, keepdims=True)
        if block:
            left = scores[:, :first]
            peak = jnp.maximum(peak, jnp.max(left, axis=1, keepdims=True))
        expo = jnp.exp2((corner - peak) * SCALE).astype(jnp.bfloat16)
        summed = jnp.dot(expo, vc[first:last, :], preferred_element_type=jnp.float32)
        if block:
            expo = jnp.exp2((left - peak) * SCALE).astype(jnp.bfloat16)
            summed = summed + jnp.dot(expo, vc[:first, :], preferred_element_type=jnp.float32)
        o_ref[first:last, :] = summed[:, :DH] / summed[:, DH:]


def softmax_part(base, doc_blocks, query_rows, key_value_rows):
    return pl.pallas_call(
        softmax_body,
        grid=(PAIR // DH,),
        out_shape=jax.ShapeDtypeStruct((SPAN, PAIR), jnp.float32),
        in_specs=[
            SMEM,
            SMEM,
            pl.BlockSpec((SPAN, DH), lambda h: (0, h)),
            pl.BlockSpec((SPAN, DH), lambda h: (0, h)),
            pl.BlockSpec((SPAN, DH), lambda h: (0, h + PAIR // DH)),
        ],
        out_specs=pl.BlockSpec((SPAN, DH), lambda h: (0, h)),
        scratch_shapes=[pltpu.VMEM((SPAN, 2 * DH), jnp.bfloat16)] * 3,
        cost_estimate=pl.CostEstimate(
            flops=4 * SPAN * SPAN * PAIR,
            bytes_accessed=SPAN * PAIR * 10,
            transcendentals=SPAN * SPAN,
        ),
        compiler_params=pltpu.CompilerParams(vmem_limit_bytes=LIMIT),
        name="softmax",
    )(base, doc_blocks, query_rows, key_value_rows, key_value_rows)


def doc_of(token, blocks_ref):
    doc = jnp.int32(0)
    total = jnp.int32(0)
    for place in range(NDOC - 1):
        total = total + blocks_ref[place] * BLOCK
        doc = doc + (token >= total).astype(jnp.int32)
    return doc


def merge_body(backs, has_own, base_ref, blocks_ref, *refs):
    base = base_ref[0]
    doc = doc_of(base + SPAN - 1 if has_own else base, blocks_ref)
    out = refs[-1]
    total = refs[-2][...] if has_own else jnp.zeros(out.shape, jnp.float32)
    for back, ref in zip(backs, refs):
        there = base - (back - 1) * SPAN - 1
        joined = (there >= 0) & (doc_of(there, blocks_ref) == doc)
        total = total + jnp.where(joined, ref[...], 0.0)
    out[...] = total


def merge(backs, has_own, base, doc_blocks, received, *own):
    return pl.pallas_call(
        functools.partial(merge_body, backs, has_own),
        out_shape=jax.ShapeDtypeStruct((PAIR, DH), jnp.float32),
        in_specs=[SMEM, SMEM] + [VMEM] * (len(received) + len(own)),
        out_specs=VMEM,
        compiler_params=pltpu.CompilerParams(vmem_limit_bytes=LIMIT),
        cost_estimate=pl.CostEstimate(
            flops=len(backs) * PAIR * DH, bytes_accessed=len(backs) * PAIR * DH * 4, transcendentals=0
        ),
        name="merge",
    )(base, doc_blocks, *received, *own)


def join_body(base_ref, blocks_ref, q_ref, soft_ref, state_ref, o_ref):
    limit = jnp.int32(0)
    total = jnp.int32(0)
    for doc in range(NDOC):
        total = total + blocks_ref[doc] * BLOCK
        limit = jnp.where(limit > 0, limit, total - base_ref[0])
    state = state_ref[...]
    high = state.astype(jnp.bfloat16)
    low = (state - high.astype(jnp.float32)).astype(jnp.bfloat16)
    both = jnp.concatenate([high, low], axis=1)
    parts = jnp.dot(q_ref[...], both, preferred_element_type=jnp.float32)
    linear = parts[:, :DH] + parts[:, DH:]
    normed = linear * lax.rsqrt(jnp.mean(linear * linear, axis=1, keepdims=True) + 1e-06)
    token = pl.program_id(1) * o_ref.shape[0] + lax.broadcasted_iota(jnp.int32, linear.shape, 0)
    normed = jnp.where(token < limit, normed, 0.0)
    o_ref[...] = (soft_ref[...] + normed).astype(jnp.bfloat16)


def join(base, doc_blocks, query_rows, soft, state):
    step = 1024
    tile = pl.BlockSpec((step, DH), lambda h, i: (i, h))
    return pl.pallas_call(
        join_body,
        grid=(PAIR // DH, SPAN // step),
        out_shape=jax.ShapeDtypeStruct((SPAN, PAIR), jnp.bfloat16),
        in_specs=[SMEM, SMEM, tile, tile, pl.BlockSpec((DH, DH), lambda h, i: (h, 0))],
        out_specs=tile,
        cost_estimate=pl.CostEstimate(
            flops=4 * SPAN * PAIR * DH, bytes_accessed=SPAN * PAIR * 8, transcendentals=0
        ),
        compiler_params=pltpu.CompilerParams(vmem_limit_bytes=LIMIT),
        name="join",
    )(base, doc_blocks, query_rows, soft, state)


def increment_body(base_ref, blocks_ref, k_ref, v_ref, o_ref):
    start = jnp.int32(0)
    total = jnp.int32(0)
    for doc in range(NDOC - 1):
        total = total + blocks_ref[doc] * BLOCK
        start = jnp.where(total - base_ref[0] < SPAN, total, start)
    token = lax.broadcasted_iota(jnp.int32, (SPAN, DH), 0)
    zero = jnp.zeros((SPAN, DH), jnp.bfloat16)
    tail = jnp.where(token >= start - base_ref[0], k_ref[...], zero)
    o_ref[...] = lax.dot_general(
        tail, v_ref[...], (((0,), (0,)), ((), ())), preferred_element_type=jnp.float32
    )


def increment(base, doc_blocks, key_value_rows):
    return pl.pallas_call(
        increment_body,
        grid=(PAIR // DH,),
        out_shape=jax.ShapeDtypeStruct((PAIR, DH), jnp.float32),
        in_specs=[
            SMEM,
            SMEM,
            pl.BlockSpec((SPAN, DH), lambda h: (0, h)),
            pl.BlockSpec((SPAN, DH), lambda h: (0, h + PAIR // DH)),
        ],
        out_specs=pl.BlockSpec((DH, DH), lambda h: (h, 0)),
        cost_estimate=pl.CostEstimate(
            flops=2 * SPAN * PAIR * DH, bytes_accessed=SPAN * PAIR * 4, transcendentals=0
        ),
        compiler_params=pltpu.CompilerParams(vmem_limit_bytes=LIMIT),
        name="increment",
    )(base, doc_blocks, key_value_rows, key_value_rows)


def on_device(queries, keys, values, doc_blocks):
    me = lax.axis_index("seq").astype(jnp.int32)
    base = me * SPAN
    key_value = to_heads(pack(keys, values))
    query_rows = to_heads(pack(queries))

    own = increment(base[None], doc_blocks, key_value)

    def from_back(value, back):
        return lax.ppermute(value, "seq", [(c, c + back) for c in range(N_SEQ - back)])

    near = (1, 8, 9)
    pieces = merge(near, True, base[None], doc_blocks, [from_back(own, b) for b in near], own)
    far = (1, 3, 5, 7)
    state = merge(far, False, base[None], doc_blocks, [from_back(pieces, b) for b in far])

    soft = softmax_part(base[None], doc_blocks, query_rows, key_value)
    mixed = join(base[None], doc_blocks, query_rows, soft, state)
    result = lax.all_to_all(
        mixed.reshape(N_HEAD, HERE, PAIR), "head", split_axis=0, concat_axis=0, tiled=True
    )
    return result.transpose(1, 0, 2).reshape(HERE, H * DH)


def solution(mesh):
    placed = (P(("seq", "head"), None), P(("seq", "head"), None), P(("seq", "head"), None), P())
    return jax.shard_map(
        on_device, mesh=mesh, in_specs=placed, out_specs=P(("seq", "head"), None), check_vma=False
    )
```
